32 devices in a mesh: grp: 2 (over y), bus: 4 (over z), line: 2 (over x), scen: 2 (over core).
Axes of the slice: x: 2, y: 2, z: 4, core: 2. Of those that a mesh axis runs over, the one named last changes fastest.
Arguments:
- injections: float32 [128, 4, 4096], P(('grp', 'bus', 'scen'), None, 'line'), parts along dimension 0, may hold values from -6 to 6
- shift_factors: float32 [8192, 16384], P('line', 'bus'), may hold values from -0.046875 to 0.046875
- line_limits: int32 [8192], P('line'), may hold values from 20 to 149
- overload_cost: float32 [8192], P('line'), may hold values from 0.5 to 5
Outputs:
- line_flows: float32 [128, 8192], P(('grp', 'bus', 'scen'), 'line'), parts along dimension 0
- penalty_gradient: float32 [128, 4, 4096], P(('grp', 'bus', 'scen'), None, 'line'), parts along dimension 0
The draws below stay inside these ranges and needn't reach their ends.
There are 2 independent parts, one for each index of `grp`. The reference program is written for one: setup_inputs(seed, part) draws one part's arguments, and reference() takes and returns one part's arrays. A program takes and returns all parts, laid end to end along the dimension named above; an argument that names none is the same for every part. Nothing has to cross between parts.
Inputs may be any that keep to these rules, and one draw needn't show every extreme that they name: `line_limits`: thermal limits in MW on a 100 MW base.
All inputs are finite; a program needn't handle non-finite values.
Results may differ from the reference program's by a relative error of at most 0.00011.
Values sent between devices are 32-bit elements; how exact they have to be, the bound alone decides.
No kernel may reach another device: no remote copies, remote signals or barrier semaphores. Data moves between devices by JAX's collectives and lax.ppermute only.
A program may use at most 128 MiB of HBM per device.

```python
import math
import jax
import jax.numpy as jnp
from jax import lax

B = 16384
L = 8192
S = 64
BSHARD = 4096
N_BUS = 4


def set_ends(array, key, smallest, high):
    extent = array.shape
    spot = [jax.random.randint(jax.random.fold_in(key, axis), (), 0, extent[axis]) for axis in range(len(extent))]
    array = array.at[tuple(spot)].set(smallest)
    longest = extent.index(max(extent))
    spot[longest] = (spot[longest] + 1) % extent[longest]
    return array.at[tuple(spot)].set(high)


def block_scale(key, shape, shards, smallest, high):
    loudness, own = 1.0, jax.random.fold_in(key, 6)
    for axis_at, blocks in shards:
        draws = jnp.exp(jax.random.uniform(jax.random.fold_in(own, axis_at), (blocks,), jnp.float32, smallest / len(shards), high / len(shards)))
        loudness = loudness * jnp.repeat(draws, shape[axis_at] // blocks).reshape([-1 if axis == axis_at else 1 for axis in range(len(shape))])
    return loudness


def normal_values(own_key, dims, spread, most, cuts=(), held_as=jnp.bfloat16):
    values = jax.random.normal(own_key, dims, jnp.float32) * spread
    if len(cuts) > 0:
        values = block_scale(own_key, dims, cuts, -0.22, 0.18) * values
    return jnp.clip(values, min=-most, max=most).astype(held_as)


def setup_inputs(seed: int = 0, part: int = 0) -> dict:
    key_list = jax.random.split(jax.random.key(seed), 5)
    part_splits = jax.random.split(jax.random.fold_in(key_list[4], part), 5)
    return {
        "injections": normal_values(part_splits[0], (S, N_BUS, BSHARD), 1.0, 6.0, ((0, 8), (2, 2)), jnp.float32),
        "shift_factors": normal_values(key_list[1], (L, B), B ** -0.5, 0.046875, ((0, 2), (1, 4)), jnp.float32),
        "line_limits": set_ends(jax.random.randint(key_list[2], (L,), 20, 150), jax.random.fold_in(key_list[2], 1), 20, 149).astype(jnp.int32),
        "overload_cost": jnp.clip(jnp.exp(math.log(5.0) - 2.3025851 * jax.random.uniform(key_list[3], (L,), jnp.float32) ** block_scale(key_list[3], (L,), ((0, 2),), -0.2, 0.2)), 0.5, 5.0),
    }


def reference(injections, shift_factors, line_limits, overload_cost):
    rows = injections.reshape(S, B)
    line_flows = jnp.dot(rows, shift_factors.T, precision=lax.Precision.HIGHEST, preferred_element_type=jnp.float32)
    limits = line_limits.astype(jnp.float32) / 100.0
    excess = jax.nn.relu(line_flows - limits) - jax.nn.relu(-line_flows - limits)
    slopes = 2.0 * overload_cost * excess
    gradient = jnp.dot(slopes, shift_factors, precision=lax.Precision.HIGHEST, preferred_element_type=jnp.float32)
    return line_flows, gradient.reshape(S, N_BUS, BSHARD)
```

```python
import functools

import jax
import jax.numpy as jnp
from jax import lax
from jax.experimental import pallas as pl
from jax.experimental.pallas import tpu as pltpu
from jax.sharding import PartitionSpec as P


F32, BF16 = jnp.float32, jnp.bfloat16
VMEM = pltpu.VMEM
MIB = 1 << 20


def in_vmem():
    return pl.BlockSpec(memory_space=pltpu.VMEM)


def halves(x):
    hi = x.astype(BF16)
    return hi, (x - hi.astype(F32)).astype(BF16)


def call(body, outs, name, args, flops=0, bytes_accessed=0, limit=4 * MIB, aliases=None):
    several = isinstance(outs, (list, tuple))
    return pl.pallas_call(
        body,
        out_shape=list(outs) if several else outs,
        in_specs=[in_vmem()] * len(args),
        out_specs=[in_vmem()] * len(outs) if several else in_vmem(),
        compiler_params=pltpu.CompilerParams(vmem_limit_bytes=limit),
        cost_estimate=pl.CostEstimate(flops=flops, bytes_accessed=bytes_accessed, transcendentals=0),
        input_output_aliases=aliases or {},
        name=name,
    )(*args)


def shaped(*shape):
    return jax.ShapeDtypeStruct(shape, F32)


def pinned(x):
    return pltpu.with_memory_space_constraint(x, pltpu.VMEM)


def pack_body(n, x_ref, *out_refs):
    me = lax.axis_index("bus")
    blocks = [x_ref[:, k, :] for k in range(n)]
    for d, out_ref in enumerate(out_refs):
        want = lax.rem(me + d, n)
        block = blocks[0]
        for k in range(1, n):
            block = jnp.where(want == k, blocks[k], block)
        out_ref[...] = block


def load_body(first, per_core, step, depth, w_ref, hi_ref, lo_ref, buf, sem):
    lines = hi_ref.shape[0]
    base = lax.axis_index("scen") * per_core + first
    count = lines // step

    def copy(c, slot):
        rows = pl.ds(pl.multiple_of(base + c * step, step), step)
        return pltpu.make_async_copy(w_ref.at[rows], buf.at[slot], sem.at[slot])

    for c in range(min(depth, count)):
        copy(c, c).start()

    @pl.loop(0, count)
    def _(c):
        slot = lax.rem(c, depth)
        copy(c, slot).wait()

        @pl.loop(0, step // 16)
        def _(r):
            at = pl.multiple_of(r * 16, 16)
            hi, lo = halves(buf[slot, pl.ds(at, 16), :])
            to = pl.ds(pl.multiple_of(c * step + at, 16), 16)
            hi_ref[to, :] = hi
            lo_ref[to, :] = lo

        @pl.when(c + depth < count)
        def _():
            copy(c + depth, slot).start()


def load(w, first, lines, per_core):
    buses = w.shape[1]
    step = min(128, lines)
    depth = min(4, lines // step)
    return pl.pallas_call(
        functools.partial(load_body, first, per_core, step, depth),
        out_shape=[VMEM((lines, buses), BF16)] * 2,
        in_specs=[pl.BlockSpec(memory_space=pltpu.HBM)],
        out_specs=[in_vmem()] * 2,
        scratch_shapes=[VMEM((depth, step, buses), F32), pltpu.SemaphoreType.DMA((depth,))],
        compiler_params=pltpu.CompilerParams(vmem_limit_bytes=depth * step * buses * 4 + 2 * MIB),
        cost_estimate=pl.CostEstimate(flops=0, bytes_accessed=lines * buses * 4, transcendentals=0),
        name="load",
    )(w)


NT = (((1,), (1,)), ((), ()))
NN = (((1,), (0,)), ((), ()))


def product(x2, xh, hi, lo, dims):
    rows = xh.shape[0]
    wide = lax.dot_general(x2, hi, dims, preferred_element_type=F32)
    narrow = lax.dot_general(xh, lo, dims, preferred_element_type=F32)
    return wide[:rows] + wide[rows:] + narrow


def doubled(x):
    hi, lo = halves(x)
    return jnp.concatenate([hi, lo], 0), hi


def tile_of(n):
    return min(256, n)


def flows_start_body(width, own_ref, other_ref, *refs):
    chunks = len(refs) // 3
    part = lax.axis_index("line")
    cols = pl.ds(pl.multiple_of(part * width, width), width)
    x2, xh = doubled(jnp.concatenate([own_ref[...], other_ref[...]], 0))
    for c in range(chunks):
        hi_ref, lo_ref, out_ref = refs[2 * c], refs[2 * c + 1], refs[2 * chunks + c]
        lines = hi_ref.shape[0]
        for j in range(0, lines, tile_of(lines)):
            at = slice(j, j + tile_of(lines))
            out_ref[:, at] = product(x2, xh, hi_ref[at, cols], lo_ref[at, cols], NT)


def flows_end_body(width, parts, groups, *refs):
    acc_ref, hi_ref, lo_ref = refs[:3]
    pairs, out_refs = refs[3 : 3 + 2 * (parts - 1)], refs[3 + 2 * (parts - 1) :]
    part = lax.axis_index("line")
    lines = hi_ref.shape[0]
    xs = [doubled(jnp.concatenate([pairs[2 * m][...], pairs[2 * m + 1][...]], 0)) for m in range(parts - 1)]
    half = acc_ref.shape[0] // 2
    size = half // groups
    for j in range(0, lines, tile_of(lines)):
        at = slice(j, j + tile_of(lines))
        total = acc_ref[:, at]
        for m in range(1, parts):
            cols = pl.ds(pl.multiple_of(lax.rem(part + parts - m, parts) * width, width), width)
            total = total + product(*xs[m - 1], hi_ref[at, cols], lo_ref[at, cols], NT)
        for e, out_ref in enumerate(out_refs):
            out_ref[:size, at] = total[e * size : (e + 1) * size]
            out_ref[size:, at] = total[half + e * size : half + (e + 1) * size]


def slopes_body(groups, *refs):
    limit_ref, price_ref = refs[groups : groups + 2]
    mine_ref, theirs_ref, slope_ref = refs[groups + 2 :]
    flows = refs[0][...]
    for ref in refs[1:groups]:
        flows = flows + ref[...]
    size = mine_ref.shape[0]
    mine_ref[...] = flows[:size]
    theirs_ref[...] = flows[size:]
    limit = limit_ref[...]
    excess = jax.nn.relu(flows - limit) - jax.nn.relu(-flows - limit)
    slope_ref[...] = price_ref[...] * excess


def gradient_body(width, parts, groups, first, which, *refs):
    hi_ref, lo_ref = refs[:2]
    slope_refs = refs[2 : 2 + groups]
    refs = refs[2 + groups :]
    acc_refs, out_refs = ((), refs) if first else (refs[: len(which)], refs[len(which) :])
    part = lax.axis_index("line")
    size = slope_refs[0].shape[0] // 2
    rows = [ref[:size] for ref in slope_refs] + [ref[size:] for ref in slope_refs]
    x2, xh = doubled(jnp.concatenate(rows, 0))
    tile = tile_of(width)
    split = len(out_refs) == 2 * len(which)
    half = size * groups
    for i, m in enumerate(which):
        begin = lax.rem(part + m, parts) * width
        for j in range(0, width, tile):
            cols = pl.ds(pl.multiple_of(begin + j, tile), tile)
            at = slice(j, j + tile)
            total = product(x2, xh, hi_ref[:, cols], lo_ref[:, cols], NN)
            if not first:
                total = total + acc_refs[i][:, at]
            if split:
                out_refs[2 * i][:, at] = total[:half]
                out_refs[2 * i + 1][:, at] = total[half:]
            else:
                out_refs[i][:, at] = total


def add_body(a_ref, b_ref, o_ref):
    o_ref[...] = a_ref[...] + b_ref[...]


def add_split_body(n, *refs):
    total = refs[0][...]
    for ref in refs[1:n]:
        total = total + ref[...]
    size = refs[n].shape[0]
    for e, out_ref in enumerate(refs[n:]):
        out_ref[...] = total[e * size : (e + 1) * size]


def unpack_body(n, *refs):
    out_ref = refs[n]
    me = lax.axis_index("bus")
    blocks = [ref[...] for ref in refs[:n]]
    for k in range(n):
        block = blocks[0]
        for e in range(1, n):
            block = jnp.where(lax.rem(me + e, n) == k, blocks[e], block)
        out_ref[:, k, :] = block


def join_flows_body(chunks, *refs):
    out_ref = refs[2 * chunks]
    me = lax.axis_index("scen")
    lines = refs[0].shape[1]
    span = lines * chunks
    for t in range(2):
        base = lax.rem(me + t, 2) * span
        for c in range(chunks):
            at = pl.ds(pl.multiple_of(base + c * lines, lines), lines)
            out_ref[:, at] = refs[t * chunks + c][...]


def shift(x, axis, by):
    n = lax.axis_size(axis)
    return lax.ppermute(x, axis, [(i, (i + by) % n) for i in range(n)])


def on_device(injections, shift_factors, line_limits, overload_cost):
    n_bus, n_line, n_scen = (lax.axis_size(a) for a in ("bus", "line", "scen"))
    own, _, width = injections.shape
    lines, buses = shift_factors.shape
    per_core = lines // n_scen
    chunks = 4
    span = per_core // chunks
    rows = own * n_bus * n_scen
    half = own * n_bus

    blocks = call(functools.partial(pack_body, n_bus), [shaped(own, width)] * n_bus, "pack", [injections])
    arrived = [blocks[0]] + [shift(blocks[d], "bus", d) for d in range(1, n_bus)]
    w = [load(shift_factors, c * span, span, per_core) for c in range(chunks)]

    first = lax.axis_index("scen") * per_core
    limits = lax.dynamic_slice_in_dim(line_limits, first, per_core).astype(F32) / 100.0
    prices = 2.0 * lax.dynamic_slice_in_dim(overload_cost, first, per_core)
    limits, prices = limits.reshape(chunks, 1, span), prices.reshape(chunks, 1, span)

    mine = jnp.concatenate(arrived, 0)
    pairs = [(mine, shift(mine, "scen", 1))]
    for m in range(1, n_line):
        far = shift(mine, "line", m)
        pairs.append((far, shift(far, "scen", 1)))

    w = [(pinned(hi), pinned(lo)) for hi, lo in w]
    flat = [x for pair in w for x in pair]
    begun = call(
        functools.partial(flows_start_body, width),
        [shaped(rows, span)] * chunks,
        "flows_start",
        [*pairs[0], *flat],
        flops=6 * rows * width * per_core,
        limit=8 * MIB,
    )
    rest = [x for pair in pairs[1:] for x in pair]
    mine_flows, theirs_flows, slopes = [], [], []
    for c in range(chunks):
        groups = call(
            functools.partial(flows_end_body, width, n_line, n_bus),
            [shaped(2 * own, span)] * n_bus,
            "flows_end",
            [begun[c], *w[c], *rest],
            flops=6 * rows * width * (n_line - 1) * span,
            limit=8 * MIB,
        )
        summands = [groups[0]] + [shift(groups[e], "bus", n_bus - e) for e in range(1, n_bus)]
        a, b, slope = call(
            functools.partial(slopes_body, n_bus),
            [shaped(own, span), shaped(own, span), shaped(2 * own, span)],
            "slopes",
            [*summands, limits[c], prices[c]],
        )
        mine_flows.append(a)
        theirs_flows.append(b)
        slopes.append([slope] + [shift(slope, "bus", e) for e in range(1, n_bus)])

    from_other = shift(jnp.concatenate(theirs_flows, 1), "scen", 1)
    from_other = [from_other[:, c * span : (c + 1) * span] for c in range(chunks)]
    line_flows = call(
        functools.partial(join_flows_body, chunks), shaped(own, lines), "join_flows", [*mine_flows, *from_other]
    )

    order = list(range(1, n_line)) + [0]
    acc = []
    for c in range(chunks - 1):
        acc = call(
            functools.partial(gradient_body, width, n_line, n_bus, c == 0, order),
            [shaped(rows, width)] * n_line,
            "gradient",
            [*w[c], *slopes[c], *acc],
            flops=6 * rows * span * buses,
            limit=8 * MIB,
            aliases={2 + n_bus + i: i for i in range(n_line)} if c else None,
        )
    sums = []
    for i, m in enumerate(order):
        keep, give = call(
            functools.partial(gradient_body, width, n_line, n_bus, False, [m]),
            [shaped(half, width)] * 2,
            "gradient_end",
            [*w[-1], *slopes[-1], acc[i]],
            flops=6 * rows * span * width,
            limit=8 * MIB,
        )
        got = shift(give, "scen", 1)
        if m:
            sums.append(shift(call(add_body, shaped(half, width), "add", [keep, got]), "line", m))
        else:
            sums += [keep, got]
    groups = call(
        functools.partial(add_split_body, len(sums)), [shaped(own, width)] * n_bus, "add_split", sums
    )
    home = [groups[0]] + [shift(groups[e], "bus", n_bus - e) for e in range(1, n_bus)]
    penalty_gradient = call(
        functools.partial(unpack_body, n_bus), shaped(own, n_bus, width), "unpack", home
    )
    return line_flows, penalty_gradient


def solution(mesh):
    in_specs = (P(("grp", "bus", "scen"), None, "line"), P("line", "bus"), P("line"), P("line"))
    out_specs = (P(("grp", "bus", "scen"), "line"), P(("grp", "bus", "scen"), None, "line"))
    return jax.shard_map(
        on_device, mesh=mesh, in_specs=in_specs, out_specs=out_specs, check_vma=False
    )
```
